256 devices in a mesh: rep: 32 (over z_hi, x, core), own: 8 (over z_lo, y).
Axes of the slice: x: 4, y: 4, z: 8 (z_hi: 4, z_lo: 2; z = z_hi * 2 + z_lo), core: 2. Of those that a mesh axis runs over, the one named last changes fastest.
Arguments:
- grads: bfloat16 [32, 8, 1024, 1024], P('rep', 'own'), may hold values from -4 to 4, as said below
- owners: int32 [8], replicated, may hold values from 0 to 7, as said below
- left_stats: float32 [8, 3, 1024, 1024], P('own', None, 'rep'), may hold values from -6 to 6
- right_stats: float32 [8, 3, 1024, 1024], P('own', None, 'rep'), may hold values from -6 to 6
- left_root: bfloat16 [8, 3, 1024, 1024], P('own', None, 'rep'), may hold values from -1 to 2
- right_root: bfloat16 [8, 3, 1024, 1024], P('own', None, 'rep'), may hold values from -1 to 2
- slot_weights: float32 [8, 3, 1024, 1024], P('own', None, 'rep'), may hold values from -6 to 6
- slot_second: float32 [8, 3, 1024, 1024], P('own', None, 'rep'), may hold values from 0.01 to 1
- norm_grads: bfloat16 [32, 8448], P('rep'), may hold values from -6 to 6
- norm_weights: float32 [8448], replicated, may hold values from 0.5 to 1.5
- norm_second: float32 [8448], replicated, may hold values from 0.01 to 1
Outputs:
- new_weights: float32 [8, 1024, 1024], P('own')
- new_left: float32 [8, 3, 1024, 1024], P('own', None, 'rep')
- new_right: float32 [8, 3, 1024, 1024], P('own', None, 'rep')
- new_second: float32 [8, 3, 1024, 1024], P('own', None, 'rep')
- new_norms: float32 [8448], replicated
- new_norm_second: float32 [8448], replicated
The draws below stay inside these ranges and needn't reach their ends.
Inputs may be any that keep to these rules, and one draw needn't show every extreme that they name: `owners`: each owner holds at most 3 blocks, and some owner holds exactly 3. `grads`: every entry is a multiple of 1/64.
All inputs are finite; a program needn't handle non-finite values.
Results may differ from the reference program's by a relative error of at most 0.0054.
Values may be sent and summed in bfloat16 or wider, within the bound.
A program may use at most 128 MiB of HBM per device.

```python
import math
import jax
import jax.numpy as jnp
from jax import lax

BLOCK = 1024
OWNERS = 8
REPLICAS = 32
NBLK = 8
SLOTS = 3
NORMW = 8448


def draw_owners(key, part):
    key_busy, key_order, key_shift = jax.random.split(key, 3)
    others = max(OWNERS - 1, 1)
    busiest = jax.random.randint(key_busy, (), 0, OWNERS)
    order = jax.random.permutation(key_order, NBLK)
    ranks = jnp.argsort(order)
    offset = jax.random.randint(key_shift, (), 0, others)
    spread = (busiest + 1 + (ranks - SLOTS + offset) % others) % OWNERS
    return jnp.where(ranks < SLOTS, busiest, spread).astype(jnp.int32)


def draw_grads(key, part):
    key_own, key_pair = jax.random.split(jax.random.fold_in(key, 5), 2)
    shape = (REPLICAS, NBLK, BLOCK, BLOCK)
    height = jnp.arange(BLOCK, dtype=jnp.float32) / BLOCK
    slab = jnp.arange(BLOCK) // (BLOCK // REPLICAS)
    pairing = jax.random.permutation(key_pair, REPLICAS)
    spike = jnp.where(slab[None, :] == pairing[:, None], 3.0, 1.0)
    base = jnp.clip(jax.random.normal(key_own, shape, jnp.float32), -6.0, 6.0)
    rise = 3.0 ** height
    scale = 0.18 * rise[None, :] * spike
    values = jnp.clip(base * scale[:, None, :, None], -3.98, 3.98)
    values = jnp.floor(values * 64.0 + 0.5) / 64.0
    return values.astype(jnp.bfloat16)


def root_draw(key):
    shape = (OWNERS, SLOTS, BLOCK, BLOCK)
    noise = jnp.clip(jax.random.normal(key, shape, jnp.float32), -3.0, 3.0)
    diagonal = (jnp.arange(BLOCK)[:, None] == jnp.arange(BLOCK)[None, :]).astype(jnp.float32)
    return (diagonal + noise * (0.7 / math.sqrt(BLOCK))).astype(jnp.bfloat16)


def draw_left_root(key, part):
    return root_draw(jax.random.fold_in(key, 11))


def draw_right_root(key, part):
    return root_draw(jax.random.fold_in(key, 23))


def spiked(entries, own_key, source, target, shards_of, factor):
    owner, partner = [(jnp.arange(entries.shape[position]) // (entries.shape[position] // shards_of)).reshape([-1 if axis == position else 1 for axis in range(entries.ndim)]) for position in (source, target)]
    chosen = jax.random.permutation(own_key, shards_of)[partner]
    strong = (owner == chosen) | (owner == (partner + shards_of // 2) % shards_of)
    return jnp.where(strong, factor * entries, entries)


def levels(key, extent, cuts, smallest, top_value):
    level = 1.0
    for axis_at, blocks in cuts:
        draws = jax.random.uniform(jax.random.fold_in(jax.random.fold_in(key, 6), axis_at), (blocks,), jnp.float32, smallest / len(cuts), top_value / len(cuts))
        level = level * jnp.repeat(jnp.exp(draws), extent[axis_at] // blocks).reshape((-1,) + (1,) * (len(extent) - 1 - axis_at))
    return level


def centred(key, shape, deviation, bound, pieces=(), kind=jnp.bfloat16):
    gain = levels(key, shape, pieces, -0.22, 0.18) if pieces else 1.0
    values = jax.random.normal(key, shape, jnp.float32) * deviation * gain
    return jnp.minimum(jnp.maximum(values, -bound), bound).astype(kind)


def bell_draw_with(rng, dims, scale, most, shards, heavy, kind=jnp.bfloat16):
    result = scale * jax.random.normal(rng, dims, jnp.float32)
    if shards:
        result = result * levels(rng, dims, shards, -0.22, 0.18)
    return jnp.clip(spiked(result, jax.random.fold_in(rng, 3), *heavy), -most, most).astype(kind)


def setup_inputs(seed: int = 0) -> dict:
    streams_of = jax.random.split(jax.random.key(seed), 12)
    return {
        "grads": draw_grads(jax.random.fold_in(streams_of[11], 71), 0),
        "owners": draw_owners(jax.random.fold_in(streams_of[11], 71), 0),
        "left_stats": centred(streams_of[2], (OWNERS, SLOTS, BLOCK, BLOCK), 1.0, 6.0, ((0, 8), (2, 32)), jnp.float32),
        "right_stats": centred(streams_of[3], (OWNERS, SLOTS, BLOCK, BLOCK), 1.0, 6.0, ((0, 8), (2, 32)), jnp.float32),
        "left_root": draw_left_root(jax.random.fold_in(streams_of[11], 71), 0),
        "right_root": draw_right_root(jax.random.fold_in(streams_of[11], 71), 0),
        "slot_weights": centred(streams_of[6], (OWNERS, SLOTS, BLOCK, BLOCK), 1.0, 6.0, ((0, 8), (2, 32)), jnp.float32),
        "slot_second": jnp.clip(jnp.exp(math.log(1.0) - 4.6051702 * jax.random.uniform(streams_of[7], (OWNERS, SLOTS, BLOCK, BLOCK), jnp.float32) ** levels(streams_of[7], (OWNERS, SLOTS, BLOCK, BLOCK), ((0, 8), (2, 32)), -0.2, 0.2)), 0.01, 1.0),
        "norm_grads": bell_draw_with(streams_of[8], (REPLICAS, NORMW), 0.3, 6.0, ((0, 32),), (0, 1, 32, 2.75)),
        "norm_weights": jnp.clip(1.0 + 0.1 * jax.random.normal(streams_of[9], (NORMW,), jnp.float32), 0.5, 1.5),
        "norm_second": jnp.clip(jnp.exp(jax.random.uniform(streams_of[10], (NORMW,), jnp.float32, math.log(0.01), math.log(1.0))), 0.01, 1.0),
    }


STAT_DECAY = 0.95
MOMENT_DECAY = 0.95
STEP_SIZE = 0.1
ADAM_EPS = 1e-08
GRAFT_EPS = 1e-06

def slot_numbers(owners):
    length = owners.shape[0]
    positions = jnp.arange(length, dtype=jnp.int32)
    same_owner = owners[:, None] == owners[None, :]
    before = positions[None, :] < positions[:, None]
    return lax.optimization_barrier(jnp.sum((same_owner & before).astype(jnp.int32), axis=1)).astype(jnp.int32)

def reference(grads, owners, left_stats, right_stats, left_root, right_root, slot_weights, slot_second, norm_grads, norm_weights, norm_second):

    def add_replica(replica, running):
        return running + lax.dynamic_index_in_dim(grads, replica, 0, keepdims=False).astype(jnp.float32)
    summed = lax.fori_loop(0, REPLICAS, add_replica, jnp.zeros(grads.shape[1:], jnp.float32))
    grad_all = summed.astype(jnp.bfloat16)
    slot_index = slot_numbers(owners)
    owner_count = left_stats.shape[0]
    slot_count = left_stats.shape[1]
    flat_count = owner_count * slot_count

    def flatten(array):
        return array.reshape((flat_count,) + array.shape[2:])

    def one_slot(inputs):
        slot_id, left_old, right_old, left_fac, right_fac, weight_old, second_old = inputs
        owner_id = slot_id // slot_count
        which = slot_id % slot_count
        chosen = ((owners == owner_id) & (slot_index == which)).astype(jnp.float32)
        grad_slot = jnp.tensordot(chosen, grad_all.astype(jnp.float32), 1).astype(jnp.bfloat16)
        new_left = STAT_DECAY * left_old + (1.0 - STAT_DECAY) / BLOCK * jnp.dot(grad_slot, grad_slot.T, preferred_element_type=jnp.float32)
        new_right = STAT_DECAY * right_old + (1.0 - STAT_DECAY) / BLOCK * jnp.dot(grad_slot.T, grad_slot, preferred_element_type=jnp.float32)
        applied = jnp.dot(left_fac, grad_slot, preferred_element_type=jnp.float32)
        direction = jnp.dot(applied, right_fac.astype(jnp.float32), precision=lax.Precision.HIGHEST)
        grad_f = grad_slot.astype(jnp.float32)
        new_second = MOMENT_DECAY * second_old + (1.0 - MOMENT_DECAY) * grad_f * grad_f
        adam_step = grad_f / (jnp.sqrt(new_second) + ADAM_EPS)
        graft_scale = jnp.sqrt(jnp.mean(adam_step * adam_step)) / jnp.sqrt(jnp.mean(direction * direction) + GRAFT_EPS)
        updated = weight_old - STEP_SIZE * graft_scale * direction
        return (new_left, new_right, new_second, updated)
    slot_ids = jnp.arange(flat_count, dtype=jnp.int32)
    new_left, new_right, new_second, updated = lax.map(one_slot, (slot_ids, flatten(left_stats), flatten(right_stats), flatten(left_root), flatten(right_root), flatten(slot_weights), flatten(slot_second)))
    target = (owners * slot_count + slot_index).astype(jnp.int32)
    new_weights = jnp.take(updated, target, axis=0)
    norm_sum = lax.optimization_barrier(jnp.sum(norm_grads.astype(jnp.float32), axis=0))
    norm_moment = MOMENT_DECAY * norm_second + (1.0 - MOMENT_DECAY) * norm_sum * norm_sum
    new_norms = norm_weights - STEP_SIZE * norm_sum / (jnp.sqrt(norm_moment) + ADAM_EPS)
    shape_back = left_stats.shape
    return (new_weights, new_left.reshape(shape_back), new_right.reshape(shape_back), new_second.reshape(shape_back), new_norms, norm_moment)
```

```python
import jax
import jax.numpy as jnp
from jax import lax
from jax.sharding import PartitionSpec as P

STAT_DECAY = 0.95
MOMENT_DECAY = 0.95
STEP_SIZE = 0.1
ADAM_EPS = 1e-08
GRAFT_EPS = 1e-06


def slot_numbers(owners):
    length = owners.shape[0]
    positions = jnp.arange(length, dtype=jnp.int32)
    same_owner = owners[:, None] == owners[None, :]
    before = positions[None, :] < positions[:, None]
    return jnp.sum((same_owner & before).astype(jnp.int32), axis=1)


def shards(
    grads,
    owners,
    left_stats,
    right_stats,
    left_root,
    right_root,
    slot_weights,
    slot_second,
    norm_grads,
    norm_weights,
    norm_second,
):
    own_here = lax.axis_index("own")
    rep_here = lax.axis_index("rep")
    blk_local = grads.shape[1]
    block_size = grads.shape[3]
    slot_count = left_stats.shape[1]
    row_count = left_stats.shape[2]
    slot_index = slot_numbers(owners)
    target = owners * slot_count + slot_index
    slot_range = jnp.arange(slot_count, dtype=jnp.int32)
    rep_count = block_size // row_count
    norm_all = lax.all_gather(norm_grads[0], "rep", axis=0, tiled=False)
    norm_sum = jnp.sum(norm_all.astype(jnp.float32), axis=0)
    grad_rows = grads[0, 0].astype(jnp.float32).reshape(rep_count, row_count, block_size)
    summed = lax.psum_scatter(grad_rows, "rep", scatter_dimension=0, tiled=False)
    grad_held = lax.optimization_barrier(summed).astype(jnp.bfloat16)[None]
    shard_part = lax.all_gather(grad_held, "own", axis=0, tiled=True)
    wanted = (owners[None, :] == own_here) & (slot_index[None, :] == slot_range[:, None])
    owned_grad = jnp.einsum(
        "ki,irc->krc", wanted.astype(jnp.bfloat16), shard_part, preferred_element_type=jnp.float32
    ).astype(jnp.bfloat16)
    left_rows = left_root[0]
    shard_part = lax.all_gather(owned_grad, "rep", axis=1, tiled=True)
    products = jnp.einsum(
        "src,snc->srn", owned_grad, shard_part, preferred_element_type=jnp.float32
    )
    left_part = products
    mine_cols = lax.dynamic_slice_in_dim(shard_part, rep_here * row_count, row_count, 2)
    right_part = jnp.einsum(
        "snr,snc->src", mine_cols, shard_part, preferred_element_type=jnp.float32
    )
    accumulate_applied = jnp.einsum(
        "srn,snc->src", left_rows, shard_part, preferred_element_type=jnp.float32
    )
    left_part, right_part, applied = (left_part, right_part, accumulate_applied)
    shard_part = lax.all_gather(right_root[0], "rep", axis=1, tiled=True)
    direction = jnp.einsum(
        "srn,snc->src", applied, shard_part.astype(jnp.float32), precision=lax.Precision.HIGHEST
    )
    grad_f = owned_grad.astype(jnp.float32)
    new_second = MOMENT_DECAY * slot_second[0] + (1.0 - MOMENT_DECAY) * grad_f * grad_f
    adam_step = grad_f / (jnp.sqrt(new_second) + ADAM_EPS)
    adam_sq = jnp.sum(adam_step * adam_step, axis=(1, 2))
    dir_sq = jnp.sum(direction * direction, axis=(1, 2))
    sq_all = lax.all_gather(jnp.stack([adam_sq, dir_sq]), "rep", axis=0, tiled=False)
    adam_total, dir_total = jnp.sum(sq_all, axis=0)
    cell_count = float(block_size * block_size)
    graft_scale = jnp.sqrt(adam_total / cell_count) / jnp.sqrt(dir_total / cell_count + GRAFT_EPS)
    updated = slot_weights[0] - STEP_SIZE * graft_scale[:, None, None] * direction
    mine_target = lax.dynamic_slice_in_dim(target, own_here * blk_local, blk_local)
    shard_part = lax.all_gather(updated, "own", axis=0, tiled=True)
    length = shard_part.shape[0]
    wanted = mine_target[:, None] == jnp.arange(length, dtype=jnp.int32)[None, :]
    held_rows = jnp.einsum(
        "ji,irc->jrc", wanted.astype(jnp.float32), shard_part, precision=lax.Precision.HIGHEST
    )
    new_weights = lax.all_gather(held_rows, "rep", axis=1, tiled=True)
    new_left = STAT_DECAY * left_stats[0] + (1.0 - STAT_DECAY) / block_size * left_part
    new_right = STAT_DECAY * right_stats[0] + (1.0 - STAT_DECAY) / block_size * right_part
    norm_moment = MOMENT_DECAY * norm_second + (1.0 - MOMENT_DECAY) * norm_sum * norm_sum
    new_norms = norm_weights - STEP_SIZE * norm_sum / (jnp.sqrt(norm_moment) + ADAM_EPS)
    return (new_weights, new_left[None], new_right[None], new_second[None], new_norms, norm_moment)


def solution(mesh):
    in_specs = (
        P("rep", "own", None, None),
        P(),
        P("own", None, "rep", None),
        P("own", None, "rep", None),
        P("own", None, "rep", None),
        P("own", None, "rep", None),
        P("own", None, "rep", None),
        P("own", None, "rep", None),
        P("rep", None),
        P(),
        P(),
    )
    out_specs = (
        P("own", None, None),
        P("own", None, "rep", None),
        P("own", None, "rep", None),
        P("own", None, "rep", None),
        P(),
        P(),
    )
    return jax.shard_map(shards, mesh=mesh, in_specs=in_specs, out_specs=out_specs, check_vma=False)
```

```python
import jax
import jax.numpy as jnp
from jax import lax
from jax.sharding import PartitionSpec as P

STAT_DECAY = 0.95
MOMENT_DECAY = 0.95
STEP_SIZE = 0.1
ADAM_EPS = 1e-08
GRAFT_EPS = 1e-06


def slot_numbers(owners):
    length = owners.shape[0]
    positions = jnp.arange(length, dtype=jnp.int32)
    same_owner = owners[:, None] == owners[None, :]
    before = positions[None, :] < positions[:, None]
    return jnp.sum((same_owner & before).astype(jnp.int32), axis=1)


def rep_gather(value, rep_count):
    rep_here = lax.axis_index("rep")
    sizes = (rep_count // 8, 4, 2)
    strides = (8, 2, 1)
    bundle = value[None]
    for size, stride in zip(sizes, strides):
        coord = (rep_here // stride) % size
        parts = [bundle]
        for shift in range(1, size):
            pairs = []
            for j in range(rep_count):
                u = (j // stride) % size
                pairs.append((j, j + ((u + shift) % size - u) * stride))
            parts.append(lax.ppermute(bundle, "rep", pairs))
        stacked = jnp.stack(parts)
        order = (coord - jnp.arange(size, dtype=jnp.int32)) % size
        bundle = jnp.take(stacked, order, axis=0).reshape((size * bundle.shape[0],) + bundle.shape[1:])
    return bundle.reshape((2, 4, rep_count // 8) + value.shape)


def shards(
    grads,
    owners,
    left_stats,
    right_stats,
    left_root,
    right_root,
    slot_weights,
    slot_second,
    norm_grads,
    norm_weights,
    norm_second,
):
    own_here = lax.axis_index("own")
    rep_here = lax.axis_index("rep")
    blk_local = grads.shape[1]
    block_size = grads.shape[3]
    slot_count = left_stats.shape[1]
    row_count = left_stats.shape[2]
    slot_index = slot_numbers(owners)
    target = owners * slot_count + slot_index
    slot_range = jnp.arange(slot_count, dtype=jnp.int32)
    rep_count = block_size // row_count
    norm_all = rep_gather(norm_grads[0], rep_count)
    norm_sum = jnp.sum(norm_all.astype(jnp.float32), axis=(0, 1, 2))
    right_all = rep_gather(right_root[0], rep_count)
    grad_rows = grads[0, 0].astype(jnp.float32).reshape(rep_count, row_count, block_size)
    summed = lax.psum_scatter(grad_rows, "rep", scatter_dimension=0, tiled=False)
    grad_held = lax.optimization_barrier(summed).astype(jnp.bfloat16)[None]
    shard_part = lax.all_gather(grad_held, "own", axis=0, tiled=True)
    wanted = (owners[None, :] == own_here) & (slot_index[None, :] == slot_range[:, None])
    owned_grad = jnp.einsum(
        "ki,irc->krc", wanted.astype(jnp.bfloat16), shard_part, preferred_element_type=jnp.float32
    ).astype(jnp.bfloat16)
    left_rows = left_root[0]
    shard_part = lax.all_gather(owned_grad, "rep", axis=1, tiled=True)
    products = jnp.einsum(
        "src,snc->srn", owned_grad, shard_part, preferred_element_type=jnp.float32
    )
    left_part = products
    mine_cols = lax.dynamic_slice_in_dim(shard_part, rep_here * row_count, row_count, 2)
    right_part = jnp.einsum(
        "snr,snc->src", mine_cols, shard_part, preferred_element_type=jnp.float32
    )
    accumulate_applied = jnp.einsum(
        "srn,snc->src", left_rows, shard_part, preferred_element_type=jnp.float32
    )
    left_part, right_part, applied = (left_part, right_part, accumulate_applied)
    applied_parts = applied.reshape(applied.shape[:2] + (rep_count // 8, 4, 2, row_count))
    direction = jnp.einsum(
        "smzxcr,cxzsrk->smk", applied_parts, right_all.astype(jnp.float32), precision=lax.Precision.HIGHEST
    )
    grad_f = owned_grad.astype(jnp.float32)
    new_second = MOMENT_DECAY * slot_second[0] + (1.0 - MOMENT_DECAY) * grad_f * grad_f
    adam_step = grad_f / (jnp.sqrt(new_second) + ADAM_EPS)
    adam_sq = jnp.sum(adam_step * adam_step, axis=(1, 2))
    dir_sq = jnp.sum(direction * direction, axis=(1, 2))
    sq_all = rep_gather(jnp.stack([adam_sq, dir_sq]), rep_count)
    adam_total, dir_total = jnp.sum(sq_all, axis=(0, 1, 2))
    cell_count = float(block_size * block_size)
    graft_scale = jnp.sqrt(adam_total / cell_count) / jnp.sqrt(dir_total / cell_count + GRAFT_EPS)
    updated = slot_weights[0] - STEP_SIZE * graft_scale[:, None, None] * direction
    mine_target = lax.dynamic_slice_in_dim(target, own_here * blk_local, blk_local)
    shard_part = lax.all_gather(updated, "own", axis=0, tiled=True)
    length = shard_part.shape[0]
    wanted = mine_target[:, None] == jnp.arange(length, dtype=jnp.int32)[None, :]
    held_rows = jnp.einsum(
        "ji,irc->jrc", wanted.astype(jnp.float32), shard_part, precision=lax.Precision.HIGHEST
    )
    new_weights = lax.all_gather(held_rows, "rep", axis=1, tiled=True)
    new_left = STAT_DECAY * left_stats[0] + (1.0 - STAT_DECAY) / block_size * left_part
    new_right = STAT_DECAY * right_stats[0] + (1.0 - STAT_DECAY) / block_size * right_part
    norm_moment = MOMENT_DECAY * norm_second + (1.0 - MOMENT_DECAY) * norm_sum * norm_sum
    new_norms = norm_weights - STEP_SIZE * norm_sum / (jnp.sqrt(norm_moment) + ADAM_EPS)
    return (new_weights, new_left[None], new_right[None], new_second[None], new_norms, norm_moment)


def solution(mesh):
    in_specs = (
        P("rep", "own", None, None),
        P(),
        P("own", None, "rep", None),
        P("own", None, "rep", None),
        P("own", None, "rep", None),
        P("own", None, "rep", None),
        P("own", None, "rep", None),
        P("own", None, "rep", None),
        P("rep", None),
        P(),
        P(),
    )
    out_specs = (
        P("own", None, None),
        P("own", None, "rep", None),
        P("own", None, "rep", None),
        P("own", None, "rep", None),
        P(),
        P(),
    )
    return jax.shard_map(shards, mesh=mesh, in_specs=in_specs, out_specs=out_specs, check_vma=False)
```

```python
import jax
import jax.numpy as jnp
from jax import lax
from jax.sharding import PartitionSpec as P

STAT_DECAY = 0.95
MOMENT_DECAY = 0.95
STEP_SIZE = 0.1
ADAM_EPS = 1e-08
GRAFT_EPS = 1e-06


def slot_numbers(owners):
    length = owners.shape[0]
    positions = jnp.arange(length, dtype=jnp.int32)
    same_owner = owners[:, None] == owners[None, :]
    before = positions[None, :] < positions[:, None]
    return jnp.sum((same_owner & before).astype(jnp.int32), axis=1)


def rep_gather(value, rep_count):
    rep_here = lax.axis_index("rep")
    sizes = (rep_count // 8, 4, 2)
    strides = (8, 2, 1)
    bundle = value[None]
    for size, stride in zip(sizes, strides):
        coord = (rep_here // stride) % size
        parts = [bundle]
        for shift in range(1, size):
            pairs = []
            for j in range(rep_count):
                u = (j // stride) % size
                pairs.append((j, j + ((u + shift) % size - u) * stride))
            parts.append(lax.ppermute(bundle, "rep", pairs))
        stacked = jnp.stack(parts)
        order = (coord - jnp.arange(size, dtype=jnp.int32)) % size
        bundle = jnp.take(stacked, order, axis=0).reshape((size * bundle.shape[0],) + bundle.shape[1:])
    return bundle.reshape((2, 4, rep_count // 8) + value.shape)


def own_gather(value, own_count):
    own_here = lax.axis_index("own")
    parts = [value]
    for shift in range(1, own_count):
        pairs = [(j, (j + shift) % own_count) for j in range(own_count)]
        parts.append(lax.ppermute(value, "own", pairs))
    stacked = jnp.stack(parts)
    order = (own_here - jnp.arange(own_count, dtype=jnp.int32)) % own_count
    return jnp.take(stacked, order, axis=0)


def own_route(slots, owners, slot_index, own_count):
    own_here = lax.axis_index("own")
    parts = [lax.dynamic_index_in_dim(slots, slot_index[own_here], 0, keepdims=False)]
    for shift in range(1, own_count):
        pairs = [(j, (j + shift) % own_count) for j in range(own_count)]
        dest = (own_here + shift) % own_count
        chunk = lax.dynamic_index_in_dim(slots, slot_index[dest], 0, keepdims=False)
        parts.append(lax.ppermute(chunk, "own", pairs))
    stacked = jnp.stack(parts)
    source_shift = (own_here - owners[own_here]) % own_count
    return lax.dynamic_index_in_dim(stacked, source_shift, 0, keepdims=True)


def shards(
    grads,
    owners,
    left_stats,
    right_stats,
    left_root,
    right_root,
    slot_weights,
    slot_second,
    norm_grads,
    norm_weights,
    norm_second,
):
    own_here = lax.axis_index("own")
    rep_here = lax.axis_index("rep")
    blk_local = grads.shape[1]
    block_size = grads.shape[3]
    slot_count = left_stats.shape[1]
    row_count = left_stats.shape[2]
    slot_index = slot_numbers(owners)
    target = owners * slot_count + slot_index
    slot_range = jnp.arange(slot_count, dtype=jnp.int32)
    rep_count = block_size // row_count
    norm_all = rep_gather(norm_grads[0], rep_count)
    norm_sum = jnp.sum(norm_all.astype(jnp.float32), axis=(0, 1, 2))
    right_all = rep_gather(right_root[0], rep_count)
    grad_rows = grads[0, 0].astype(jnp.float32).reshape(rep_count, row_count, block_size)
    summed = lax.psum_scatter(grad_rows, "rep", scatter_dimension=0, tiled=False)
    grad_held = lax.optimization_barrier(summed).astype(jnp.bfloat16)[None]
    own_count = owners.shape[0] // blk_local
    shard_part = own_gather(grad_held[0], own_count)
    wanted = (owners[None, :] == own_here) & (slot_index[None, :] == slot_range[:, None])
    owned_grad = jnp.einsum(
        "ki,irc->krc", wanted.astype(jnp.bfloat16), shard_part, preferred_element_type=jnp.float32
    ).astype(jnp.bfloat16)
    left_rows = left_root[0]
    shard_part = lax.all_gather(owned_grad, "rep", axis=1, tiled=True)
    products = jnp.einsum(
        "src,snc->srn", owned_grad, shard_part, preferred_element_type=jnp.float32
    )
    left_part = products
    mine_cols = lax.dynamic_slice_in_dim(shard_part, rep_here * row_count, row_count, 2)
    right_part = jnp.einsum(
        "snr,snc->src", mine_cols, shard_part, preferred_element_type=jnp.float32
    )
    accumulate_applied = jnp.einsum(
        "srn,snc->src", left_rows, shard_part, preferred_element_type=jnp.float32
    )
    left_part, right_part, applied = (left_part, right_part, accumulate_applied)
    applied_parts = applied.reshape(applied.shape[:2] + (rep_count // 8, 4, 2, row_count))
    direction = jnp.einsum(
        "smzxcr,cxzsrk->smk", applied_parts, right_all.astype(jnp.float32), precision=lax.Precision.HIGHEST
    )
    grad_f = owned_grad.astype(jnp.float32)
    new_second = MOMENT_DECAY * slot_second[0] + (1.0 - MOMENT_DECAY) * grad_f * grad_f
    adam_step = grad_f / (jnp.sqrt(new_second) + ADAM_EPS)
    adam_sq = jnp.sum(adam_step * adam_step, axis=(1, 2))
    dir_sq = jnp.sum(direction * direction, axis=(1, 2))
    sq_all = rep_gather(jnp.stack([adam_sq, dir_sq]), rep_count)
    adam_total, dir_total = jnp.sum(sq_all, axis=(0, 1, 2))
    cell_count = float(block_size * block_size)
    graft_scale = jnp.sqrt(adam_total / cell_count) / jnp.sqrt(dir_total / cell_count + GRAFT_EPS)
    updated = slot_weights[0] - STEP_SIZE * graft_scale[:, None, None] * direction
    held_rows = own_route(updated, owners, slot_index, own_count)
    new_weights = lax.all_gather(held_rows, "rep", axis=1, tiled=True)
    new_left = STAT_DECAY * left_stats[0] + (1.0 - STAT_DECAY) / block_size * left_part
    new_right = STAT_DECAY * right_stats[0] + (1.0 - STAT_DECAY) / block_size * right_part
    norm_moment = MOMENT_DECAY * norm_second + (1.0 - MOMENT_DECAY) * norm_sum * norm_sum
    new_norms = norm_weights - STEP_SIZE * norm_sum / (jnp.sqrt(norm_moment) + ADAM_EPS)
    return (new_weights, new_left[None], new_right[None], new_second[None], new_norms, norm_moment)


def solution(mesh):
    in_specs = (
        P("rep", "own", None, None),
        P(),
        P("own", None, "rep", None),
        P("own", None, "rep", None),
        P("own", None, "rep", None),
        P("own", None, "rep", None),
        P("own", None, "rep", None),
        P("own", None, "rep", None),
        P("rep", None),
        P(),
        P(),
    )
    out_specs = (
        P("own", None, None),
        P("own", None, "rep", None),
        P("own", None, "rep", None),
        P("own", None, "rep", None),
        P(),
        P(),
    )
    return jax.shard_map(shards, mesh=mesh, in_specs=in_specs, out_specs=out_specs, check_vma=False)
```

```python
import jax
import jax.numpy as jnp
from jax import lax
from jax.sharding import PartitionSpec as P

STAT_DECAY = 0.95
MOMENT_DECAY = 0.95
STEP_SIZE = 0.1
ADAM_EPS = 1e-08
GRAFT_EPS = 1e-06


def slot_numbers(owners):
    length = owners.shape[0]
    positions = jnp.arange(length, dtype=jnp.int32)
    same_owner = owners[:, None] == owners[None, :]
    before = positions[None, :] < positions[:, None]
    return jnp.sum((same_owner & before).astype(jnp.int32), axis=1)


def rep_gather(value, rep_count):
    rep_here = lax.axis_index("rep")
    sizes = (rep_count // 8, 4, 2)
    strides = (8, 2, 1)
    bundle = value[None]
    for size, stride in zip(sizes, strides):
        coord = (rep_here // stride) % size
        parts = [bundle]
        for shift in range(1, size):
            pairs = []
            for j in range(rep_count):
                u = (j // stride) % size
                pairs.append((j, j + ((u + shift) % size - u) * stride))
            parts.append(lax.ppermute(bundle, "rep", pairs))
        stacked = jnp.stack(parts)
        order = (coord - jnp.arange(size, dtype=jnp.int32)) % size
        bundle = jnp.take(stacked, order, axis=0).reshape((size * bundle.shape[0],) + bundle.shape[1:])
    return bundle.reshape((2, 4, rep_count // 8) + value.shape)


def own_route(slots, owners, slot_index, own_count):
    own_here = lax.axis_index("own")
    parts = [lax.dynamic_index_in_dim(slots, slot_index[own_here], 0, keepdims=False)]
    for shift in range(1, own_count):
        pairs = [(j, (j + shift) % own_count) for j in range(own_count)]
        dest = (own_here + shift) % own_count
        chunk = lax.dynamic_index_in_dim(slots, slot_index[dest], 0, keepdims=False)
        parts.append(lax.ppermute(chunk, "own", pairs))
    stacked = jnp.stack(parts)
    source_shift = (own_here - owners[own_here]) % own_count
    return lax.dynamic_index_in_dim(stacked, source_shift, 0, keepdims=True)


def shards(
    grads,
    owners,
    left_stats,
    right_stats,
    left_root,
    right_root,
    slot_weights,
    slot_second,
    norm_grads,
    norm_weights,
    norm_second,
):
    own_here = lax.axis_index("own")
    rep_here = lax.axis_index("rep")
    blk_local = grads.shape[1]
    block_size = grads.shape[3]
    slot_count = left_stats.shape[1]
    row_count = left_stats.shape[2]
    slot_index = slot_numbers(owners)
    target = owners * slot_count + slot_index
    slot_range = jnp.arange(slot_count, dtype=jnp.int32)
    rep_count = block_size // row_count
    norm_all = rep_gather(norm_grads[0], rep_count)
    norm_sum = jnp.sum(norm_all.astype(jnp.float32), axis=(0, 1, 2))
    right_all = rep_gather(right_root[0], rep_count)
    grad_rows = grads[0, 0].astype(jnp.float32).reshape(rep_count, row_count, block_size)
    summed = lax.psum_scatter(grad_rows, "rep", scatter_dimension=0, tiled=False)
    grad_held = lax.optimization_barrier(summed).astype(jnp.bfloat16)[None]
    shard_part = lax.all_gather(grad_held, "own", axis=0, tiled=True)
    wanted = (owners[None, :] == own_here) & (slot_index[None, :] == slot_range[:, None])
    owned_grad = jnp.einsum(
        "ki,irc->krc", wanted.astype(jnp.bfloat16), shard_part, preferred_element_type=jnp.float32
    ).astype(jnp.bfloat16)
    left_rows = left_root[0]
    shard_part = lax.all_gather(owned_grad, "rep", axis=1, tiled=True)
    products = jnp.einsum(
        "src,snc->srn", owned_grad, shard_part, preferred_element_type=jnp.float32
    )
    left_part = products
    mine_cols = lax.dynamic_slice_in_dim(shard_part, rep_here * row_count, row_count, 2)
    right_part = jnp.einsum(
        "snr,snc->src", mine_cols, shard_part, preferred_element_type=jnp.float32
    )
    accumulate_applied = jnp.einsum(
        "srn,snc->src", left_rows, shard_part, preferred_element_type=jnp.float32
    )
    left_part, right_part, applied = (left_part, right_part, accumulate_applied)
    applied_parts = applied.reshape(applied.shape[:2] + (rep_count // 8, 4, 2, row_count))
    direction = jnp.einsum(
        "smzxcr,cxzsrk->smk", applied_parts, right_all.astype(jnp.float32), precision=lax.Precision.HIGHEST
    )
    grad_f = owned_grad.astype(jnp.float32)
    new_second = MOMENT_DECAY * slot_second[0] + (1.0 - MOMENT_DECAY) * grad_f * grad_f
    adam_step = grad_f / (jnp.sqrt(new_second) + ADAM_EPS)
    adam_sq = jnp.sum(adam_step * adam_step, axis=(1, 2))
    dir_sq = jnp.sum(direction * direction, axis=(1, 2))
    own_count = owners.shape[0] // blk_local
    weight_rows = own_route(slot_weights[0], owners, slot_index, own_count)
    direction_all = lax.all_gather(direction, "own", axis=0, tiled=True)
    direction_rows = lax.dynamic_index_in_dim(direction_all, target[own_here], 0, keepdims=True)
    sq_all = rep_gather(jnp.stack([adam_sq, dir_sq]), rep_count)
    sq_total = jnp.sum(sq_all, axis=(0, 1, 2))
    sq_owners = lax.all_gather(sq_total, "own", axis=0, tiled=False)
    sq_mine = lax.dynamic_index_in_dim(sq_owners, owners[own_here], 0, keepdims=False)
    adam_total = sq_mine[0, slot_index[own_here]]
    dir_total = sq_mine[1, slot_index[own_here]]
    cell_count = float(block_size * block_size)
    graft_scale = jnp.sqrt(adam_total / cell_count) / jnp.sqrt(dir_total / cell_count + GRAFT_EPS)
    held_rows = weight_rows - STEP_SIZE * graft_scale * direction_rows
    new_weights = lax.all_gather(held_rows, "rep", axis=1, tiled=True)
    new_left = STAT_DECAY * left_stats[0] + (1.0 - STAT_DECAY) / block_size * left_part
    new_right = STAT_DECAY * right_stats[0] + (1.0 - STAT_DECAY) / block_size * right_part
    norm_moment = MOMENT_DECAY * norm_second + (1.0 - MOMENT_DECAY) * norm_sum * norm_sum
    new_norms = norm_weights - STEP_SIZE * norm_sum / (jnp.sqrt(norm_moment) + ADAM_EPS)
    return (new_weights, new_left[None], new_right[None], new_second[None], new_norms, norm_moment)


def solution(mesh):
    in_specs = (
        P("rep", "own", None, None),
        P(),
        P("own", None, "rep", None),
        P("own", None, "rep", None),
        P("own", None, "rep", None),
        P("own", None, "rep", None),
        P("own", None, "rep", None),
        P("own", None, "rep", None),
        P("rep", None),
        P(),
        P(),
    )
    out_specs = (
        P("own", None, None),
        P("own", None, "rep", None),
        P("own", None, "rep", None),
        P("own", None, "rep", None),
        P(),
        P(),
    )
    return jax.shard_map(shards, mesh=mesh, in_specs=in_specs, out_specs=out_specs, check_vma=False)
```

```python
import jax
import jax.numpy as jnp
from jax import lax
from jax.sharding import PartitionSpec as P

STAT_DECAY = 0.95
MOMENT_DECAY = 0.95
STEP_SIZE = 0.1
ADAM_EPS = 1e-08
GRAFT_EPS = 1e-06


def slot_numbers(owners):
    length = owners.shape[0]
    positions = jnp.arange(length, dtype=jnp.int32)
    same_owner = owners[:, None] == owners[None, :]
    before = positions[None, :] < positions[:, None]
    return jnp.sum((same_owner & before).astype(jnp.int32), axis=1)


def rep_gather(value, rep_count):
    rep_here = lax.axis_index("rep")
    sizes = (rep_count // 8, 4, 2)
    strides = (8, 2, 1)
    bundle = value[None]
    for size, stride in zip(sizes, strides):
        coord = (rep_here // stride) % size
        parts = [bundle]
        for shift in range(1, size):
            pairs = []
            for j in range(rep_count):
                u = (j // stride) % size
                pairs.append((j, j + ((u + shift) % size - u) * stride))
            parts.append(lax.ppermute(bundle, "rep", pairs))
        stacked = jnp.stack(parts)
        order = (coord - jnp.arange(size, dtype=jnp.int32)) % size
        bundle = jnp.take(stacked, order, axis=0).reshape((size * bundle.shape[0],) + bundle.shape[1:])
    return bundle.reshape((2, 4, rep_count // 8) + value.shape)


def shard_body(
    grads,
    owners,
    left_stats,
    right_stats,
    left_root,
    right_root,
    slot_weights,
    slot_second,
    norm_grads,
    norm_weights,
    norm_second,
):
    own_here = lax.axis_index("own")
    rep_here = lax.axis_index("rep")
    blk_local = grads.shape[1]
    block_size = grads.shape[3]
    slot_count = left_stats.shape[1]
    row_count = left_stats.shape[2]
    slot_index = slot_numbers(owners)
    target = owners * slot_count + slot_index
    slot_range = jnp.arange(slot_count, dtype=jnp.int32)
    rep_count = block_size // row_count
    norm_all = rep_gather(norm_grads[0], rep_count)
    norm_sum = jnp.sum(norm_all.astype(jnp.float32), axis=(0, 1, 2))
    right_all = rep_gather(right_root[0], rep_count)
    grad_rows = grads[0, 0].astype(jnp.float32).reshape(rep_count, row_count, block_size)
    summed = lax.psum_scatter(grad_rows, "rep", scatter_dimension=0, tiled=False)
    grad_held = lax.optimization_barrier(summed).astype(jnp.bfloat16)[None]
    shard_part = lax.all_gather(grad_held, "own", axis=0, tiled=True)
    wanted = (owners[None, :] == own_here) & (slot_index[None, :] == slot_range[:, None])
    owned_grad = jnp.einsum(
        "ki,irc->krc", wanted.astype(jnp.bfloat16), shard_part, preferred_element_type=jnp.float32
    ).astype(jnp.bfloat16)
    left_rows = left_root[0]
    half = block_size // 2
    part_sc = lax.all_gather(owned_grad[:, :, :half], "rep", axis=1, tiled=True)
    part_dma = rep_gather(owned_grad[:, :, half:], rep_count)
    part_dma = jnp.transpose(part_dma, (3, 2, 1, 0, 4, 5)).reshape(part_sc.shape)
    shard_part = jnp.concatenate([part_sc, part_dma], axis=2)
    products = jnp.einsum(
        "src,snc->srn", owned_grad, shard_part, preferred_element_type=jnp.float32
    )
    left_part = products
    mine_cols = lax.dynamic_slice_in_dim(shard_part, rep_here * row_count, row_count, 2)
    right_part = jnp.einsum(
        "snr,snc->src", mine_cols, shard_part, preferred_element_type=jnp.float32
    )
    accumulate_applied = jnp.einsum(
        "srn,snc->src", left_rows, shard_part, preferred_element_type=jnp.float32
    )
    left_part, right_part, applied = (left_part, right_part, accumulate_applied)
    applied_parts = applied.reshape(applied.shape[:2] + (rep_count // 8, 4, 2, row_count))
    direction = jnp.einsum(
        "smzxcr,cxzsrk->smk", applied_parts, right_all.astype(jnp.float32), precision=lax.Precision.HIGHEST
    )
    grad_f = owned_grad.astype(jnp.float32)
    new_second = MOMENT_DECAY * slot_second[0] + (1.0 - MOMENT_DECAY) * grad_f * grad_f
    adam_step = grad_f / (jnp.sqrt(new_second) + ADAM_EPS)
    adam_sq = jnp.sum(adam_step * adam_step, axis=(1, 2))
    dir_sq = jnp.sum(direction * direction, axis=(1, 2))
    sq_all = rep_gather(jnp.stack([adam_sq, dir_sq]), rep_count)
    adam_total, dir_total = jnp.sum(sq_all, axis=(0, 1, 2))
    cell_count = float(block_size * block_size)
    graft_scale = jnp.sqrt(adam_total / cell_count) / jnp.sqrt(dir_total / cell_count + GRAFT_EPS)
    updated = slot_weights[0] - STEP_SIZE * graft_scale[:, None, None] * direction
    mine_target = lax.dynamic_slice_in_dim(target, own_here * blk_local, blk_local)
    shard_part = lax.all_gather(updated, "own", axis=0, tiled=True)
    length = shard_part.shape[0]
    wanted = mine_target[:, None] == jnp.arange(length, dtype=jnp.int32)[None, :]
    held_rows = jnp.einsum(
        "ji,irc->jrc", wanted.astype(jnp.float32), shard_part, precision=lax.Precision.HIGHEST
    )
    new_weights = lax.all_gather(held_rows, "rep", axis=1, tiled=True)
    new_left = STAT_DECAY * left_stats[0] + (1.0 - STAT_DECAY) / block_size * left_part
    new_right = STAT_DECAY * right_stats[0] + (1.0 - STAT_DECAY) / block_size * right_part
    norm_moment = MOMENT_DECAY * norm_second + (1.0 - MOMENT_DECAY) * norm_sum * norm_sum
    new_norms = norm_weights - STEP_SIZE * norm_sum / (jnp.sqrt(norm_moment) + ADAM_EPS)
    return (new_weights, new_left[None], new_right[None], new_second[None], new_norms, norm_moment)


def solution(mesh):
    in_specs = (
        P("rep", "own", None, None),
        P(),
        P("own", None, "rep", None),
        P("own", None, "rep", None),
        P("own", None, "rep", None),
        P("own", None, "rep", None),
        P("own", None, "rep", None),
        P("own", None, "rep", None),
        P("rep", None),
        P(),
        P(),
    )
    out_specs = (
        P("own", None, None),
        P("own", None, "rep", None),
        P("own", None, "rep", None),
        P("own", None, "rep", None),
        P(),
        P(),
    )
    return jax.shard_map(shard_body, mesh=mesh, in_specs=in_specs, out_specs=out_specs, check_vma=False)
```

```python
import jax
import jax.numpy as jnp
from jax import lax
from jax.sharding import PartitionSpec as P

STAT_DECAY = 0.95
MOMENT_DECAY = 0.95
STEP_SIZE = 0.1
ADAM_EPS = 1e-08
GRAFT_EPS = 1e-06


def slot_numbers(owners):
    length = owners.shape[0]
    positions = jnp.arange(length, dtype=jnp.int32)
    same_owner = owners[:, None] == owners[None, :]
    before = positions[None, :] < positions[:, None]
    return jnp.sum((same_owner & before).astype(jnp.int32), axis=1)


def rep_gather(value, rep_count):
    rep_here = lax.axis_index("rep")
    sizes = (rep_count // 8, 4, 2)
    strides = (8, 2, 1)
    bundle = value[None]
    for size, stride in zip(sizes, strides):
        coord = (rep_here // stride) % size
        parts = [bundle]
        for shift in range(1, size):
            pairs = []
            for j in range(rep_count):
                u = (j // stride) % size
                pairs.append((j, j + ((u + shift) % size - u) * stride))
            parts.append(lax.ppermute(bundle, "rep", pairs))
        stacked = jnp.stack(parts)
        order = (coord - jnp.arange(size, dtype=jnp.int32)) % size
        bundle = jnp.take(stacked, order, axis=0).reshape((size * bundle.shape[0],) + bundle.shape[1:])
    return bundle.reshape((2, 4, rep_count // 8) + value.shape)


def shard_body(
    grads,
    owners,
    left_stats,
    right_stats,
    left_root,
    right_root,
    slot_weights,
    slot_second,
    norm_grads,
    norm_weights,
    norm_second,
):
    own_here = lax.axis_index("own")
    rep_here = lax.axis_index("rep")
    blk_local = grads.shape[1]
    block_size = grads.shape[3]
    slot_count = left_stats.shape[1]
    row_count = left_stats.shape[2]
    slot_index = slot_numbers(owners)
    target = owners * slot_count + slot_index
    slot_range = jnp.arange(slot_count, dtype=jnp.int32)
    rep_count = block_size // row_count
    norm_all = rep_gather(norm_grads[0], rep_count)
    norm_sum = jnp.sum(norm_all.astype(jnp.float32), axis=(0, 1, 2))
    right_all = rep_gather(right_root[0], rep_count)
    grad_rows = grads[0, 0].astype(jnp.float32).reshape(rep_count, row_count, block_size)
    summed = lax.psum_scatter(grad_rows, "rep", scatter_dimension=0, tiled=False)
    grad_held = lax.optimization_barrier(summed).astype(jnp.bfloat16)[None]
    shard_part = lax.all_gather(grad_held, "own", axis=0, tiled=True)
    wanted = (owners[None, :] == own_here) & (slot_index[None, :] == slot_range[:, None])
    owned_grad = jnp.einsum(
        "ki,irc->krc", wanted.astype(jnp.bfloat16), shard_part, preferred_element_type=jnp.float32
    ).astype(jnp.bfloat16)
    left_rows = left_root[0]
    half = block_size // 2
    part_sc = lax.all_gather(owned_grad[:, :, :half], "rep", axis=1, tiled=True)
    part_dma = rep_gather(owned_grad[:, :, half:], rep_count)
    part_dma = jnp.transpose(part_dma, (3, 2, 1, 0, 4, 5)).reshape(part_sc.shape)
    shard_part = jnp.concatenate([part_sc, part_dma], axis=2)
    products = jnp.einsum(
        "src,snc->srn", owned_grad, shard_part, preferred_element_type=jnp.float32
    )
    left_part = products
    mine_cols = lax.dynamic_slice_in_dim(shard_part, rep_here * row_count, row_count, 2)
    right_part = jnp.einsum(
        "snr,snc->src", mine_cols, shard_part, preferred_element_type=jnp.float32
    )
    accumulate_applied = jnp.einsum(
        "srn,snc->src", left_rows, shard_part, preferred_element_type=jnp.float32
    )
    left_part, right_part, applied = (left_part, right_part, accumulate_applied)
    applied_parts = applied.reshape(applied.shape[:2] + (rep_count // 8, 4, 2, row_count))
    direction = jnp.einsum(
        "smzxcr,cxzsrk->smk", applied_parts, right_all.astype(jnp.float32), precision=lax.Precision.HIGHEST
    )
    grad_f = owned_grad.astype(jnp.float32)
    new_second = MOMENT_DECAY * slot_second[0] + (1.0 - MOMENT_DECAY) * grad_f * grad_f
    adam_step = grad_f / (jnp.sqrt(new_second) + ADAM_EPS)
    adam_sq = jnp.sum(adam_step * adam_step, axis=(1, 2))
    dir_sq = jnp.sum(direction * direction, axis=(1, 2))
    sq_all = rep_gather(jnp.stack([adam_sq, dir_sq]), rep_count)
    adam_total, dir_total = jnp.sum(sq_all, axis=(0, 1, 2))
    cell_count = float(block_size * block_size)
    graft_scale = jnp.sqrt(adam_total / cell_count) / jnp.sqrt(dir_total / cell_count + GRAFT_EPS)
    updated = slot_weights[0] - STEP_SIZE * graft_scale[:, None, None] * direction
    mine_target = lax.dynamic_slice_in_dim(target, own_here * blk_local, blk_local)
    shard_part = lax.all_gather(updated, "own", axis=0, tiled=True)
    length = shard_part.shape[0]
    wanted = mine_target[:, None] == jnp.arange(length, dtype=jnp.int32)[None, :]
    held_rows = jnp.einsum(
        "ji,irc->jrc", wanted.astype(jnp.float32), shard_part, precision=lax.Precision.HIGHEST
    )
    weights_sc = lax.all_gather(held_rows[:, :, :half], "rep", axis=1, tiled=True)
    weights_dma = rep_gather(held_rows[:, :, half:], rep_count)
    weights_dma = jnp.transpose(weights_dma, (3, 2, 1, 0, 4, 5)).reshape(weights_sc.shape)
    new_weights = jnp.concatenate([weights_sc, weights_dma], axis=2)
    new_left = STAT_DECAY * left_stats[0] + (1.0 - STAT_DECAY) / block_size * left_part
    new_right = STAT_DECAY * right_stats[0] + (1.0 - STAT_DECAY) / block_size * right_part
    norm_moment = MOMENT_DECAY * norm_second + (1.0 - MOMENT_DECAY) * norm_sum * norm_sum
    new_norms = norm_weights - STEP_SIZE * norm_sum / (jnp.sqrt(norm_moment) + ADAM_EPS)
    return (new_weights, new_left[None], new_right[None], new_second[None], new_norms, norm_moment)


def solution(mesh):
    in_specs = (
        P("rep", "own", None, None),
        P(),
        P("own", None, "rep", None),
        P("own", None, "rep", None),
        P("own", None, "rep", None),
        P("own", None, "rep", None),
        P("own", None, "rep", None),
        P("own", None, "rep", None),
        P("rep", None),
        P(),
        P(),
    )
    out_specs = (
        P("own", None, None),
        P("own", None, "rep", None),
        P("own", None, "rep", None),
        P("own", None, "rep", None),
        P(),
        P(),
    )
    return jax.shard_map(shard_body, mesh=mesh, in_specs=in_specs, out_specs=out_specs, check_vma=False)
```

```python
import jax
import jax.numpy as jnp
from jax import lax
from jax.sharding import PartitionSpec as P

STAT_DECAY = 0.95
MOMENT_DECAY = 0.95
STEP_SIZE = 0.1
ADAM_EPS = 1e-08
GRAFT_EPS = 1e-06


def slot_numbers(owners):
    length = owners.shape[0]
    positions = jnp.arange(length, dtype=jnp.int32)
    same_owner = owners[:, None] == owners[None, :]
    before = positions[None, :] < positions[:, None]
    return jnp.sum((same_owner & before).astype(jnp.int32), axis=1)


def rep_gather(value, rep_count):
    rep_here = lax.axis_index("rep")
    sizes = (rep_count // 8, 4, 2)
    strides = (8, 2, 1)
    bundle = value[None]
    for size, stride in zip(sizes, strides):
        coord = (rep_here // stride) % size
        parts = [bundle]
        for shift in range(1, size):
            pairs = []
            for j in range(rep_count):
                u = (j // stride) % size
                pairs.append((j, j + ((u + shift) % size - u) * stride))
            parts.append(lax.ppermute(bundle, "rep", pairs))
        stacked = jnp.stack(parts)
        order = (coord - jnp.arange(size, dtype=jnp.int32)) % size
        bundle = jnp.take(stacked, order, axis=0).reshape((size * bundle.shape[0],) + bundle.shape[1:])
    return bundle.reshape((2, 4, rep_count // 8) + value.shape)


def shard_body(
    grads,
    owners,
    left_stats,
    right_stats,
    left_root,
    right_root,
    slot_weights,
    slot_second,
    norm_grads,
    norm_weights,
    norm_second,
):
    own_here = lax.axis_index("own")
    rep_here = lax.axis_index("rep")
    blk_local = grads.shape[1]
    block_size = grads.shape[3]
    slot_count = left_stats.shape[1]
    row_count = left_stats.shape[2]
    slot_index = slot_numbers(owners)
    target = owners * slot_count + slot_index
    slot_range = jnp.arange(slot_count, dtype=jnp.int32)
    rep_count = block_size // row_count
    norm_all = rep_gather(norm_grads[0], rep_count)
    norm_sum = jnp.sum(norm_all.astype(jnp.float32), axis=(0, 1, 2))
    right_all = rep_gather(right_root[0], rep_count)
    grad_rows = grads[0, 0].astype(jnp.float32).reshape(rep_count, row_count, block_size)
    summed = lax.psum_scatter(grad_rows, "rep", scatter_dimension=0, tiled=False)
    grad_held = lax.optimization_barrier(summed).astype(jnp.bfloat16)[None]
    shard_part = lax.all_gather(grad_held, "own", axis=0, tiled=True)
    wanted = (owners[None, :] == own_here) & (slot_index[None, :] == slot_range[:, None])
    owned_grad = jnp.einsum(
        "ki,irc->krc", wanted.astype(jnp.bfloat16), shard_part, preferred_element_type=jnp.float32
    ).astype(jnp.bfloat16)
    left_rows = left_root[0]
    split = slot_count - 1
    part_sc = lax.all_gather(owned_grad[:split], "rep", axis=1, tiled=True)
    part_dma = rep_gather(owned_grad[split:], rep_count)
    part_dma = jnp.transpose(part_dma, (3, 2, 1, 0, 4, 5)).reshape((slot_count - split,) + part_sc.shape[1:])
    shard_part = jnp.concatenate([part_sc, part_dma], axis=0)
    products = jnp.einsum(
        "src,snc->srn", owned_grad, shard_part, preferred_element_type=jnp.float32
    )
    left_part = products
    mine_cols = lax.dynamic_slice_in_dim(shard_part, rep_here * row_count, row_count, 2)
    right_part = jnp.einsum(
        "snr,snc->src", mine_cols, shard_part, preferred_element_type=jnp.float32
    )
    accumulate_applied = jnp.einsum(
        "srn,snc->src", left_rows, shard_part, preferred_element_type=jnp.float32
    )
    left_part, right_part, applied = (left_part, right_part, accumulate_applied)
    applied_parts = applied.reshape(applied.shape[:2] + (rep_count // 8, 4, 2, row_count))
    direction = jnp.einsum(
        "smzxcr,cxzsrk->smk", applied_parts, right_all.astype(jnp.float32), precision=lax.Precision.HIGHEST
    )
    grad_f = owned_grad.astype(jnp.float32)
    new_second = MOMENT_DECAY * slot_second[0] + (1.0 - MOMENT_DECAY) * grad_f * grad_f
    adam_step = grad_f / (jnp.sqrt(new_second) + ADAM_EPS)
    adam_sq = jnp.sum(adam_step * adam_step, axis=(1, 2))
    dir_sq = jnp.sum(direction * direction, axis=(1, 2))
    sq_all = rep_gather(jnp.stack([adam_sq, dir_sq]), rep_count)
    adam_total, dir_total = jnp.sum(sq_all, axis=(0, 1, 2))
    cell_count = float(block_size * block_size)
    graft_scale = jnp.sqrt(adam_total / cell_count) / jnp.sqrt(dir_total / cell_count + GRAFT_EPS)
    updated = slot_weights[0] - STEP_SIZE * graft_scale[:, None, None] * direction
    mine_target = lax.dynamic_slice_in_dim(target, own_here * blk_local, blk_local)
    shard_part = lax.all_gather(updated, "own", axis=0, tiled=True)
    length = shard_part.shape[0]
    wanted = mine_target[:, None] == jnp.arange(length, dtype=jnp.int32)[None, :]
    held_rows = jnp.einsum(
        "ji,irc->jrc", wanted.astype(jnp.float32), shard_part, precision=lax.Precision.HIGHEST
    )
    new_weights = lax.all_gather(held_rows, "rep", axis=1, tiled=True)
    new_left = STAT_DECAY * left_stats[0] + (1.0 - STAT_DECAY) / block_size * left_part
    new_right = STAT_DECAY * right_stats[0] + (1.0 - STAT_DECAY) / block_size * right_part
    norm_moment = MOMENT_DECAY * norm_second + (1.0 - MOMENT_DECAY) * norm_sum * norm_sum
    new_norms = norm_weights - STEP_SIZE * norm_sum / (jnp.sqrt(norm_moment) + ADAM_EPS)
    return (new_weights, new_left[None], new_right[None], new_second[None], new_norms, norm_moment)


def solution(mesh):
    in_specs = (
        P("rep", "own", None, None),
        P(),
        P("own", None, "rep", None),
        P("own", None, "rep", None),
        P("own", None, "rep", None),
        P("own", None, "rep", None),
        P("own", None, "rep", None),
        P("own", None, "rep", None),
        P("rep", None),
        P(),
        P(),
    )
    out_specs = (
        P("own", None, None),
        P("own", None, "rep", None),
        P("own", None, "rep", None),
        P("own", None, "rep", None),
        P(),
        P(),
    )
    return jax.shard_map(shard_body, mesh=mesh, in_specs=in_specs, out_specs=out_specs, check_vma=False)
```

```python
import jax
import jax.numpy as jnp
from jax import lax
from jax.sharding import PartitionSpec as P

STAT_DECAY = 0.95
MOMENT_DECAY = 0.95
STEP_SIZE = 0.1
ADAM_EPS = 1e-08
GRAFT_EPS = 1e-06


def slot_numbers(owners):
    length = owners.shape[0]
    positions = jnp.arange(length, dtype=jnp.int32)
    same_owner = owners[:, None] == owners[None, :]
    before = positions[None, :] < positions[:, None]
    return jnp.sum((same_owner & before).astype(jnp.int32), axis=1)


def rep_gather(value, rep_count):
    rep_here = lax.axis_index("rep")
    sizes = (rep_count // 8, 4, 2)
    strides = (8, 2, 1)
    bundle = value[None]
    for size, stride in zip(sizes, strides):
        coord = (rep_here // stride) % size
        parts = [bundle]
        for shift in range(1, size):
            pairs = []
            for j in range(rep_count):
                u = (j // stride) % size
                pairs.append((j, j + ((u + shift) % size - u) * stride))
            parts.append(lax.ppermute(bundle, "rep", pairs))
        stacked = jnp.stack(parts)
        order = (coord - jnp.arange(size, dtype=jnp.int32)) % size
        bundle = jnp.take(stacked, order, axis=0).reshape((size * bundle.shape[0],) + bundle.shape[1:])
    return bundle.reshape((2, 4, rep_count // 8) + value.shape)


def shard_body(
    grads,
    owners,
    left_stats,
    right_stats,
    left_root,
    right_root,
    slot_weights,
    slot_second,
    norm_grads,
    norm_weights,
    norm_second,
):
    own_here = lax.axis_index("own")
    rep_here = lax.axis_index("rep")
    block_size = grads.shape[3]
    slot_count = left_stats.shape[1]
    row_count = left_stats.shape[2]
    slot_index = slot_numbers(owners)
    target = owners * slot_count + slot_index
    slot_range = jnp.arange(slot_count, dtype=jnp.int32)
    rep_count = block_size // row_count
    norm_all = rep_gather(norm_grads[0], rep_count)
    norm_sum = jnp.sum(norm_all.astype(jnp.float32), axis=(0, 1, 2))
    right_all = rep_gather(right_root[0], rep_count)
    grad_rows = grads[0, 0].astype(jnp.float32).reshape(rep_count, row_count, block_size)
    summed = lax.psum_scatter(grad_rows, "rep", scatter_dimension=0, tiled=False)
    grad_held = lax.optimization_barrier(summed).astype(jnp.bfloat16)[None]
    weights_all = lax.all_gather(slot_weights[0], "own", axis=0, tiled=True)
    shard_part = lax.all_gather(grad_held, "own", axis=0, tiled=True)
    wanted = (owners[None, :] == own_here) & (slot_index[None, :] == slot_range[:, None])
    owned_grad = jnp.einsum(
        "ki,irc->krc", wanted.astype(jnp.bfloat16), shard_part, preferred_element_type=jnp.float32
    ).astype(jnp.bfloat16)
    left_rows = left_root[0]
    split = slot_count - 1
    part_sc = lax.all_gather(owned_grad[:split], "rep", axis=1, tiled=True)
    part_dma = rep_gather(owned_grad[split:], rep_count)
    part_dma = jnp.transpose(part_dma, (3, 2, 1, 0, 4, 5)).reshape((slot_count - split,) + part_sc.shape[1:])
    shard_part = jnp.concatenate([part_sc, part_dma], axis=0)
    products = jnp.einsum(
        "src,snc->srn", owned_grad, shard_part, preferred_element_type=jnp.float32
    )
    left_part = products
    mine_cols = lax.dynamic_slice_in_dim(shard_part, rep_here * row_count, row_count, 2)
    right_part = jnp.einsum(
        "snr,snc->src", mine_cols, shard_part, preferred_element_type=jnp.float32
    )
    accumulate_applied = jnp.einsum(
        "srn,snc->src", left_rows, shard_part, preferred_element_type=jnp.float32
    )
    left_part, right_part, applied = (left_part, right_part, accumulate_applied)
    applied_parts = applied.reshape(applied.shape[:2] + (rep_count // 8, 4, 2, row_count))
    direction = jnp.einsum(
        "smzxcr,cxzsrk->smk", applied_parts, right_all.astype(jnp.float32), precision=lax.Precision.HIGHEST
    )
    grad_f = owned_grad.astype(jnp.float32)
    new_second = MOMENT_DECAY * slot_second[0] + (1.0 - MOMENT_DECAY) * grad_f * grad_f
    adam_step = grad_f / (jnp.sqrt(new_second) + ADAM_EPS)
    adam_sq = jnp.sum(adam_step * adam_step, axis=(1, 2))
    dir_sq = jnp.sum(direction * direction, axis=(1, 2))
    direction_all = lax.all_gather(direction, "own", axis=0, tiled=True)
    sq_all = rep_gather(jnp.stack([adam_sq, dir_sq]), rep_count)
    sq_total = jnp.sum(sq_all, axis=(0, 1, 2))
    sq_owners = lax.all_gather(sq_total, "own", axis=0, tiled=False)
    sq_mine = lax.dynamic_index_in_dim(sq_owners, owners[own_here], 0, keepdims=False)
    adam_total = sq_mine[0, slot_index[own_here]]
    dir_total = sq_mine[1, slot_index[own_here]]
    cell_count = float(block_size * block_size)
    graft_scale = jnp.sqrt(adam_total / cell_count) / jnp.sqrt(dir_total / cell_count + GRAFT_EPS)
    mine = target[own_here]
    weight_rows = lax.dynamic_index_in_dim(weights_all, mine, 0, keepdims=True)
    direction_rows = lax.dynamic_index_in_dim(direction_all, mine, 0, keepdims=True)
    held_rows = weight_rows - STEP_SIZE * graft_scale * direction_rows
    new_weights = lax.all_gather(held_rows, "rep", axis=1, tiled=True)
    new_left = STAT_DECAY * left_stats[0] + (1.0 - STAT_DECAY) / block_size * left_part
    new_right = STAT_DECAY * right_stats[0] + (1.0 - STAT_DECAY) / block_size * right_part
    norm_moment = MOMENT_DECAY * norm_second + (1.0 - MOMENT_DECAY) * norm_sum * norm_sum
    new_norms = norm_weights - STEP_SIZE * norm_sum / (jnp.sqrt(norm_moment) + ADAM_EPS)
    return (new_weights, new_left[None], new_right[None], new_second[None], new_norms, norm_moment)


def solution(mesh):
    in_specs = (
        P("rep", "own", None, None),
        P(),
        P("own", None, "rep", None),
        P("own", None, "rep", None),
        P("own", None, "rep", None),
        P("own", None, "rep", None),
        P("own", None, "rep", None),
        P("own", None, "rep", None),
        P("rep", None),
        P(),
        P(),
    )
    out_specs = (
        P("own", None, None),
        P("own", None, "rep", None),
        P("own", None, "rep", None),
        P("own", None, "rep", None),
        P(),
        P(),
    )
    return jax.shard_map(shard_body, mesh=mesh, in_specs=in_specs, out_specs=out_specs, check_vma=False)
```

```python
import jax
import jax.numpy as jnp
from jax import lax
from jax.sharding import PartitionSpec as P

STAT_DECAY = 0.95
MOMENT_DECAY = 0.95
STEP_SIZE = 0.1
ADAM_EPS = 1e-08
GRAFT_EPS = 1e-06


def slot_numbers(owners):
    length = owners.shape[0]
    positions = jnp.arange(length, dtype=jnp.int32)
    same_owner = owners[:, None] == owners[None, :]
    before = positions[None, :] < positions[:, None]
    return jnp.sum((same_owner & before).astype(jnp.int32), axis=1)


def rep_gather(value, rep_count):
    rep_here = lax.axis_index("rep")
    sizes = (rep_count // 8, 4, 2)
    strides = (8, 2, 1)
    bundle = value[None]
    for size, stride in zip(sizes, strides):
        coord = (rep_here // stride) % size
        parts = [bundle]
        for shift in range(1, size):
            pairs = []
            for j in range(rep_count):
                u = (j // stride) % size
                pairs.append((j, j + ((u + shift) % size - u) * stride))
            parts.append(lax.ppermute(bundle, "rep", pairs))
        stacked = jnp.stack(parts)
        order = (coord - jnp.arange(size, dtype=jnp.int32)) % size
        bundle = jnp.take(stacked, order, axis=0).reshape((size * bundle.shape[0],) + bundle.shape[1:])
    return bundle.reshape((2, 4, rep_count // 8) + value.shape)


def own_gather_staged(value, own_count):
    own_here = lax.axis_index("own")
    bundle = value[None]
    for size, stride in ((4, 1), (own_count // 4, 4)):
        coord = (own_here // stride) % size
        parts = [bundle]
        for shift in range(1, size):
            pairs = []
            for j in range(own_count):
                u = (j // stride) % size
                pairs.append((j, j + ((u + shift) % size - u) * stride))
            parts.append(lax.ppermute(bundle, "own", pairs))
        stacked = jnp.stack(parts)
        order = (coord - jnp.arange(size, dtype=jnp.int32)) % size
        bundle = jnp.take(stacked, order, axis=0).reshape((size * bundle.shape[0],) + bundle.shape[1:])
    return bundle


def shard_body(
    grads,
    owners,
    left_stats,
    right_stats,
    left_root,
    right_root,
    slot_weights,
    slot_second,
    norm_grads,
    norm_weights,
    norm_second,
):
    own_here = lax.axis_index("own")
    rep_here = lax.axis_index("rep")
    blk_local = grads.shape[1]
    block_size = grads.shape[3]
    slot_count = left_stats.shape[1]
    row_count = left_stats.shape[2]
    slot_index = slot_numbers(owners)
    target = owners * slot_count + slot_index
    slot_range = jnp.arange(slot_count, dtype=jnp.int32)
    rep_count = block_size // row_count
    norm_all = rep_gather(norm_grads[0], rep_count)
    norm_sum = jnp.sum(norm_all.astype(jnp.float32), axis=(0, 1, 2))
    right_all = rep_gather(right_root[0], rep_count)
    grad_rows = grads[0, 0].astype(jnp.float32).reshape(rep_count, row_count, block_size)
    summed = lax.psum_scatter(grad_rows, "rep", scatter_dimension=0, tiled=False)
    grad_held = lax.optimization_barrier(summed).astype(jnp.bfloat16)[None]
    weights_all = lax.all_gather(slot_weights[0], "own", axis=0, tiled=True)
    shard_part = lax.all_gather(grad_held, "own", axis=0, tiled=True)
    wanted = (owners[None, :] == own_here) & (slot_index[None, :] == slot_range[:, None])
    owned_grad = jnp.einsum(
        "ki,irc->krc", wanted.astype(jnp.bfloat16), shard_part, preferred_element_type=jnp.float32
    ).astype(jnp.bfloat16)
    left_rows = left_root[0]
    split = slot_count - 1
    part_sc = lax.all_gather(owned_grad[:split], "rep", axis=1, tiled=True)
    part_dma = rep_gather(owned_grad[split:], rep_count)
    part_dma = jnp.transpose(part_dma, (3, 2, 1, 0, 4, 5)).reshape((slot_count - split,) + part_sc.shape[1:])
    shard_part = jnp.concatenate([part_sc, part_dma], axis=0)
    products = jnp.einsum(
        "src,snc->srn", owned_grad, shard_part, preferred_element_type=jnp.float32
    )
    left_part = products
    mine_cols = lax.dynamic_slice_in_dim(shard_part, rep_here * row_count, row_count, 2)
    right_part = jnp.einsum(
        "snr,snc->src", mine_cols, shard_part, preferred_element_type=jnp.float32
    )
    accumulate_applied = jnp.einsum(
        "srn,snc->src", left_rows, shard_part, preferred_element_type=jnp.float32
    )
    left_part, right_part, applied = (left_part, right_part, accumulate_applied)
    applied_parts = applied.reshape(applied.shape[:2] + (rep_count // 8, 4, 2, row_count))
    direction = jnp.einsum(
        "smzxcr,cxzsrk->smk", applied_parts, right_all.astype(jnp.float32), precision=lax.Precision.HIGHEST
    )
    grad_f = owned_grad.astype(jnp.float32)
    new_second = MOMENT_DECAY * slot_second[0] + (1.0 - MOMENT_DECAY) * grad_f * grad_f
    adam_step = grad_f / (jnp.sqrt(new_second) + ADAM_EPS)
    adam_sq = jnp.sum(adam_step * adam_step, axis=(1, 2))
    dir_sq = jnp.sum(direction * direction, axis=(1, 2))
    direction_all = lax.all_gather(direction, "own", axis=0, tiled=True)
    sq_all = rep_gather(jnp.stack([adam_sq, dir_sq]), rep_count)
    sq_total = jnp.sum(sq_all, axis=(0, 1, 2))
    sq_owners = own_gather_staged(sq_total, owners.shape[0] // blk_local)
    sq_mine = lax.dynamic_index_in_dim(sq_owners, owners[own_here], 0, keepdims=False)
    adam_total = sq_mine[0, slot_index[own_here]]
    dir_total = sq_mine[1, slot_index[own_here]]
    cell_count = float(block_size * block_size)
    graft_scale = jnp.sqrt(adam_total / cell_count) / jnp.sqrt(dir_total / cell_count + GRAFT_EPS)
    mine = target[own_here]
    weight_rows = lax.dynamic_index_in_dim(weights_all, mine, 0, keepdims=True)
    direction_rows = lax.dynamic_index_in_dim(direction_all, mine, 0, keepdims=True)
    held_rows = weight_rows - STEP_SIZE * graft_scale * direction_rows
    new_weights = lax.all_gather(held_rows, "rep", axis=1, tiled=True)
    new_left = STAT_DECAY * left_stats[0] + (1.0 - STAT_DECAY) / block_size * left_part
    new_right = STAT_DECAY * right_stats[0] + (1.0 - STAT_DECAY) / block_size * right_part
    norm_moment = MOMENT_DECAY * norm_second + (1.0 - MOMENT_DECAY) * norm_sum * norm_sum
    new_norms = norm_weights - STEP_SIZE * norm_sum / (jnp.sqrt(norm_moment) + ADAM_EPS)
    return (new_weights, new_left[None], new_right[None], new_second[None], new_norms, norm_moment)


def solution(mesh):
    in_specs = (
        P("rep", "own", None, None),
        P(),
        P("own", None, "rep", None),
        P("own", None, "rep", None),
        P("own", None, "rep", None),
        P("own", None, "rep", None),
        P("own", None, "rep", None),
        P("own", None, "rep", None),
        P("rep", None),
        P(),
        P(),
    )
    out_specs = (
        P("own", None, None),
        P("own", None, "rep", None),
        P("own", None, "rep", None),
        P("own", None, "rep", None),
        P(),
        P(),
    )
    return jax.shard_map(shard_body, mesh=mesh, in_specs=in_specs, out_specs=out_specs, check_vma=False)
```
